32 devices in a mesh: tm: 16 (over z, y, x), region: 2 (over core).
Axes of the slice: x: 2, y: 2, z: 4, core: 2. Of those that a mesh axis runs over, the one named last changes fastest.
Arguments:
- cost: bfloat16 [384, 24, 1024], P('tm', 'region'), may hold values from -25 to 25
- demand: bfloat16 [384, 24, 256], P('tm', 'region'), may hold values from -25 to 25
- conversion: float32 [1024, 256], replicated, may hold values from -0.1875 to 0.1875
- upper: float32 [24, 1024], P('region'), may hold values from 0.2 to 2
- decay: float32 [384, 24, 128], P('tm', 'region'), may hold values from 0.4 to 1
- energy_cap: float32 [24, 128], P('region'), may hold values from 0.02 to 0.4
- annual_cap: float32 [24, 1024], P('region'), may hold values from 0.05 to 1
- line_ends: int32 [64, 2], P('region'), may hold values from 0 to 23, as said below
- line_cap: float32 [64], P('region'), may hold values from 0.2 to 2
Outputs:
- primal: bfloat16 [384, 24, 1024], P('tm', 'region')
- flows: float32 [384, 64], P('tm', 'region')
- prices: float32 [384, 24, 256], P('tm', 'region')
- storage_dual: float32 [384, 24, 128], P('tm', 'region')
- year_dual: float32 [24, 1024], P('region')
The draws below stay inside these ranges and needn't reach their ends.
Inputs may be any that keep to these rules, and one draw needn't show every extreme that they name: `line_ends`: each line joins two different regions, every region is the first end of some line.
All inputs are finite; a program needn't handle non-finite values.
Results may differ from the reference program's by a relative error of at most 0.0012.
Values sent between devices are 32-bit elements; how exact they have to be, the bound alone decides.
A program may use at most 64 MiB of HBM per device.

```python
import math
import jax
import jax.numpy as jnp
from jax import lax

K = 1024
STORAGE_COUNT = 128
M = 256
ITERS = 2
HOURS_IN_ALL = 384
REGIONS_IN_ALL = 24
LINES = 64


def scaled_field(key, last_width):
    random_key_list = jax.random.split(key, 3)
    base = jax.random.truncated_normal(random_key_list[0], -3.0, 3.0, (HOURS_IN_ALL, REGIONS_IN_ALL, last_width), jnp.float32)
    hour_scale = jnp.exp(jax.random.uniform(random_key_list[1], (HOURS_IN_ALL, 1, 1), jnp.float32, 0.0, math.log(10.0)))
    column_scale = jnp.exp(jax.random.uniform(random_key_list[2], (1, 1, last_width), jnp.float32, 0.0, math.log(10.0)))
    ramp = jnp.exp(math.log(3.0) * jnp.arange(HOURS_IN_ALL, dtype=jnp.float32) / max(HOURS_IN_ALL - 1, 1))[:, None, None]
    return base * hour_scale * column_scale * ramp / 40.0


def draw_cost(key, part):
    return scaled_field(jax.random.fold_in(key, 11), K).astype(jnp.bfloat16)


def draw_demand(key, part):
    return scaled_field(jax.random.fold_in(key, 23), M).astype(jnp.bfloat16)


def draw_decay(key, part):
    random_key_list = jax.random.split(jax.random.fold_in(key, 37), 7)
    slow_share = 0.4
    middle_share = 0.4
    class_draw = jax.random.uniform(random_key_list[0], (REGIONS_IN_ALL, STORAGE_COUNT), jnp.float32)
    slow = class_draw < slow_share
    middle = jnp.logical_and(class_draw >= slow_share, class_draw < slow_share + middle_share)
    fast_rate = 1.0 / jax.random.uniform(random_key_list[1], (REGIONS_IN_ALL, STORAGE_COUNT), jnp.float32, 20.0, 50.0)
    slow_rate = jax.random.uniform(random_key_list[2], (REGIONS_IN_ALL, STORAGE_COUNT), jnp.float32, 0.1, 1.0) / HOURS_IN_ALL
    middle_rate = 1.0 / jax.random.uniform(random_key_list[6], (REGIONS_IN_ALL, STORAGE_COUNT), jnp.float32, 210.0, 227.0)
    region_factor = jnp.exp(jax.random.uniform(random_key_list[3], (REGIONS_IN_ALL, 1), jnp.float32, math.log(0.5), math.log(2.0)))
    rate = jnp.where(slow, slow_rate * region_factor, jnp.where(middle, middle_rate, fast_rate * region_factor))
    closing_output = jnp.broadcast_to(jnp.exp(-rate)[None], (HOURS_IN_ALL, REGIONS_IN_ALL, STORAGE_COUNT))
    spike_hours = jax.random.permutation(random_key_list[4], HOURS_IN_ALL)[:3]
    spike_keep_mask = jax.random.uniform(random_key_list[5], (3, REGIONS_IN_ALL, STORAGE_COUNT), jnp.float32, 0.6, 0.8)
    hour_index_rows = jnp.arange(HOURS_IN_ALL)
    for spike_count in range(3):
        closing_output = closing_output * jnp.where((hour_index_rows == spike_hours[spike_count])[:, None, None], spike_keep_mask[spike_count][None], 1.0)
    return closing_output


def draw_line_ends(key, part):
    random_key_list = jax.random.split(jax.random.fold_in(key, 41), 2)
    offset = jax.random.randint(random_key_list[0], (), 0, REGIONS_IN_ALL)
    first = (jnp.arange(LINES, dtype=jnp.int32) + offset) % REGIONS_IN_ALL
    second = (first + jax.random.randint(random_key_list[1], (LINES,), 1, REGIONS_IN_ALL)) % REGIONS_IN_ALL
    return jnp.stack([first, second], axis=1).astype(jnp.int32)


def block_scale(own_key, extent, cuts, smallest, high):
    level = 1.0
    for dim, blocks in cuts:
        draws = jax.random.uniform(jax.random.fold_in(jax.random.fold_in(own_key, 6), dim), (blocks,), jnp.float32, smallest / len(cuts), high / len(cuts))
        level = level * jnp.repeat(jnp.exp(draws), extent[dim] // blocks).reshape((-1,) + (1,) * (len(extent) - 1 - dim))
    return level


def normal_values(key, dims, deviation, reach, kind=jnp.bfloat16):
    return jnp.clip(deviation * jax.random.normal(key, dims, jnp.float32), -reach, reach).astype(kind)


def setup_inputs(seed: int = 0) -> dict:
    splits = jax.random.split(jax.random.key(seed), 10)
    return {
        "cost": draw_cost(jax.random.fold_in(splits[9], 71), 0),
        "demand": draw_demand(jax.random.fold_in(splits[9], 71), 0),
        "conversion": normal_values(splits[2], (K, M), K ** -0.5, 0.1875, jnp.float32),
        "upper": jnp.clip(jnp.exp(math.log(2.0) - 2.3025851 * jax.random.uniform(splits[3], (REGIONS_IN_ALL, K), jnp.float32) ** block_scale(splits[3], (REGIONS_IN_ALL, K), ((0, 2),), -0.2, 0.2)), 0.2, 2.0),
        "decay": draw_decay(jax.random.fold_in(splits[9], 71), 0),
        "energy_cap": jnp.clip(jnp.exp(math.log(0.4) - 2.9957323 * jax.random.uniform(splits[5], (REGIONS_IN_ALL, STORAGE_COUNT), jnp.float32) ** block_scale(splits[5], (REGIONS_IN_ALL, STORAGE_COUNT), ((0, 2),), -0.2, 0.2)), 0.02, 0.4),
        "annual_cap": jnp.clip(jnp.exp(math.log(1.0) - 2.9957323 * jax.random.uniform(splits[6], (REGIONS_IN_ALL, K), jnp.float32) ** block_scale(splits[6], (REGIONS_IN_ALL, K), ((0, 2),), -0.2, 0.2)), 0.05, 1.0),
        "line_ends": draw_line_ends(jax.random.fold_in(splits[9], 71), 0),
        "line_cap": jnp.clip(jnp.exp(math.log(2.0) - 2.3025851 * jax.random.uniform(splits[8], (LINES,), jnp.float32) ** block_scale(splits[8], (LINES,), ((0, 2),), -0.2, 0.2)), 0.2, 2.0),
    }


step_ratio = 0.5

def affine(earlier, later):
    return (earlier[0] * later[0], later[0] * earlier[1] + later[1])

def reference(cost, demand, conversion, upper, decay, energy_cap, annual_cap, line_ends, line_cap):
    highest = lax.Precision.HIGHEST
    level_scale = 1.0 / math.sqrt(HOURS_IN_ALL)
    year_scale = 1.0 / math.sqrt(HOURS_IN_ALL)
    year_bound = math.sqrt(HOURS_IN_ALL)
    costs = cost.astype(jnp.float32)
    loads = demand.astype(jnp.float32)
    omega = jnp.sqrt(jnp.sum(costs * costs) / jnp.sum(loads * loads))
    tau_step = step_ratio / omega
    sigma_step = step_ratio * omega
    columns = jnp.arange(K, dtype=jnp.int32)
    lower = jnp.where(columns[None, :] < STORAGE_COUNT, -upper, jnp.float32(0.0))
    region_ids = jnp.arange(REGIONS_IN_ALL, dtype=jnp.int32)
    incidence = (line_ends[:, 1:2] == region_ids[None, :]).astype(jnp.float32) - (line_ends[:, 0:1] == region_ids[None, :]).astype(jnp.float32)

    def levels_of(charge):
        scale_run, offset_run = lax.associative_scan(affine, (decay, charge), axis=0)
        return level_scale * offset_run

    def levels_adjoint(dual):
        weighted = level_scale * dual
        scale_run, offset_run = lax.associative_scan(affine, (decay, decay * weighted), axis=0, reverse=True)
        return weighted + jnp.concatenate([offset_run[1:], jnp.zeros_like(offset_run[:1])], axis=0)
    primal = jnp.zeros((HOURS_IN_ALL, REGIONS_IN_ALL, K), jnp.float32)
    flows = jnp.zeros((HOURS_IN_ALL, LINES), jnp.float32)
    prices = jnp.zeros((HOURS_IN_ALL, REGIONS_IN_ALL, M), jnp.float32)
    storage_dual = jnp.zeros((HOURS_IN_ALL, REGIONS_IN_ALL, STORAGE_COUNT), jnp.float32)
    year_dual = jnp.zeros((REGIONS_IN_ALL, K), jnp.float32)
    for step in range(ITERS):
        back = jnp.dot(prices.reshape(-1, M), conversion.T, precision=highest).reshape(HOURS_IN_ALL, REGIONS_IN_ALL, K)
        stored = levels_adjoint(storage_dual)
        stored = jnp.pad(stored, ((0, 0), (0, 0), (0, K - STORAGE_COUNT)))
        grad = costs + back + stored + year_scale * year_dual[None]
        new_primal = jnp.clip(primal - tau_step * grad, lower[None], upper[None])
        flow_grad = jnp.dot(prices[:, :, 0], incidence.T, precision=highest)
        new_flows = jnp.clip(flows - tau_step * flow_grad, -line_cap[None], line_cap[None])
        bar = 2.0 * new_primal - primal
        flow_bar = 2.0 * new_flows - flows
        inflow = jnp.dot(flow_bar, incidence, precision=highest)
        image = jnp.dot(bar.reshape(-1, K), conversion, precision=highest).reshape(HOURS_IN_ALL, REGIONS_IN_ALL, M)
        image = jnp.concatenate([image[:, :, :1] + inflow[:, :, None], image[:, :, 1:]], axis=2)
        prices = prices + sigma_step * (image - loads)
        storage_dual = jnp.maximum(storage_dual + sigma_step * (levels_of(bar[:, :, :STORAGE_COUNT]) - energy_cap[None]), 0.0)
        year_dual = jnp.maximum(year_dual + sigma_step * (year_scale * lax.optimization_barrier(jnp.sum(bar, axis=0)) - year_bound * annual_cap), 0.0)
        primal = new_primal
        flows = new_flows
    return (primal.astype(jnp.bfloat16), flows, prices, storage_dual, year_dual)
```

```python
import functools
import math

import jax
import jax.numpy as jnp
from jax import lax
from jax.experimental import pallas as pl
from jax.experimental.pallas import tpu as pltpu
from jax.sharding import PartitionSpec as P

step_ratio = 0.5
LANES = 128
SUBLANES = 8
CHUNK = 256


def up_to(value, multiple):
    return -(-value // multiple) * multiple


def padded(x, rows):
    missing = rows - x.shape[0]
    if missing == 0:
        return x
    return jnp.concatenate([x, jnp.zeros((missing,) + x.shape[1:], x.dtype)], axis=0)


def split_in_two(x):
    high = x.astype(jnp.bfloat16)
    return high, (x - high.astype(jnp.float32)).astype(jnp.bfloat16)


def product(a_high, a_low, b_high, b_low, contract_b):
    dims = (((1,), (contract_b,)), ((), ()))
    dot = functools.partial(
        lax.dot_general, dimension_numbers=dims, preferred_element_type=jnp.float32
    )
    return dot(a_high, b_high) + (dot(a_high, b_low) + dot(a_low, b_high))


def kernel(
    time_count,
    group_count,
    cost,
    demand,
    conversion,
    upper,
    decay,
    energy_cap,
    annual_cap,
    line_ends,
    line_cap,
    primal_out,
    flows_out,
    prices_out,
    storage_out,
    year_out,
    conv_high,
    conv_low,
    bar_high,
    bar_low,
    price_high,
    price_low,
    prices,
    image,
    back,
    keep,
    charge,
    levels,
    storage,
    stored,
    lower,
    year_sum,
    year_dual,
    square_recv,
    bus_recv,
    inflow_recv,
    first_send,
    first_recv,
    spread_send,
    spread_recv,
    turn_send,
    turn_recv,
    again_send,
    again_recv,
    last_send,
    last_recv,
    send_sem,
    recv_sem,
    group_send_sem,
    group_recv_sem,
):
    me = lax.axis_index("tm")
    group = lax.axis_index("region")
    regions, hours, width = cost.shape
    rows_bus = demand.shape[2]
    units = decay.shape[1]
    rows = lower.shape[0]
    pair = (2 * SUBLANES) // math.gcd(hours, 2 * SUBLANES)
    chunks = [slice(i, i + CHUNK) for i in range(0, width, CHUNK)]
    blocks = width // LANES
    tiles = (rows // SUBLANES) * blocks
    share = -(-tiles // time_count)
    hours_all = hours * time_count
    scale = 1.0 / math.sqrt(hours_all)
    year_bound = math.sqrt(hours_all)
    f32 = jnp.float32

    barrier = pltpu.get_barrier_semaphore()

    def greet_time(k, _):
        pl.semaphore_signal(
            barrier,
            inc=1,
            device_id={"tm": lax.rem(me + k, time_count)},
            device_id_type=pl.DeviceIdType.MESH,
        )
        return 0

    lax.fori_loop(1, time_count, greet_time, 0)

    def greet_group(k, _):
        pl.semaphore_signal(
            barrier,
            inc=1,
            device_id={"region": lax.rem(group + k, group_count)},
            device_id_type=pl.DeviceIdType.MESH,
        )
        return 0

    lax.fori_loop(1, group_count, greet_group, 0)

    def send_time(phase, source_of, recv):
        def one(k, _):
            peer = lax.rem(me + k, time_count)
            pltpu.make_async_remote_copy(
                src_ref=source_of(peer),
                dst_ref=recv.at[me],
                send_sem=send_sem.at[phase],
                recv_sem=recv_sem.at[phase],
                device_id={"tm": peer},
                device_id_type=pl.DeviceIdType.MESH,
            ).start()
            return 0

        lax.fori_loop(1, time_count, one, 0)

    def send_group(phase, recv):
        def one(k, _):
            pltpu.make_async_remote_copy(
                src_ref=recv.at[group],
                dst_ref=recv.at[group],
                send_sem=group_send_sem.at[phase],
                recv_sem=group_recv_sem.at[phase],
                device_id={"region": lax.rem(group + k, group_count)},
                device_id_type=pl.DeviceIdType.MESH,
            ).start()
            return 0

        lax.fori_loop(1, group_count, one, 0)

    def await_bytes(recv, count, sem):
        if count > 1:
            part = recv.at[pl.ds(0, count - 1)]
            pltpu.make_async_copy(part, part, sem).wait()

    zero_units = jnp.zeros((regions, units), f32)
    for t in range(hours):
        keep[t] = decay[pl.ds(t, regions, stride=hours), :]

    def square_sums(r, carry):
        a, b = carry
        for chunk in chunks:
            c = cost[r, :, chunk].astype(f32)
            a = a + c * c
        l = demand[r].astype(f32)
        return a, b + l * l

    a, b = lax.fori_loop(
        0,
        regions,
        square_sums,
        (jnp.zeros((hours, CHUNK), f32), jnp.zeros((hours, rows_bus), f32)),
    )
    whole_decay = lax.fori_loop(
        0, hours, lambda t, d: d * keep[t], jnp.ones((regions, units), f32)
    )

    def folded(x):
        x = jnp.sum(x, axis=0, keepdims=True)
        return sum(x[:, i * LANES : (i + 1) * LANES] for i in range(x.shape[1] // LANES))

    own_squares = padded(jnp.concatenate([folded(a), folded(b)], axis=0), SUBLANES)
    square_recv[group] = own_squares
    pl.semaphore_wait(barrier, time_count - 1 + group_count - 1)
    send_group(0, square_recv)
    column = lax.broadcasted_iota(jnp.int32, (regions, width), 1)
    lower[0:regions, :] = jnp.where(column < units, -upper[...], 0.0)
    year_sum[...] = jnp.zeros_like(year_sum)
    conv = conversion[...]
    high, low = split_in_two(conv)
    conv_high[...] = high
    conv_low[...] = low
    await_bytes(square_recv, group_count, group_recv_sem.at[0])
    squares = jnp.sum(square_recv[...], axis=0)
    first_send[0:rows, :] = padded(whole_decay, rows)
    first_send[rows : rows + SUBLANES, :] = squares
    first_recv[me, 0:rows, :] = padded(whole_decay, rows)
    first_recv[me, rows : rows + SUBLANES, :] = squares
    send_time(0, lambda peer: first_send, first_recv)

    bus_width = bus_recv.shape[2]
    ends = line_ends[...]
    region_id = lax.broadcasted_iota(jnp.int32, (bus_width, ends.shape[1]), 0)
    incidence = (ends[1:2, :] == region_id).astype(f32) - (ends[0:1, :] == region_id).astype(f32)
    spot = lax.broadcasted_iota(jnp.int32, (hours, bus_width), 1) - group * regions

    await_bytes(first_recv, time_count, recv_sem.at[0])
    squares = jnp.sum(first_recv[:, rows : rows + SUBLANES, :], axis=0)
    sums = jnp.sum(squares, axis=1, keepdims=True)
    omega = jnp.sqrt(sums[0:1] / sums[1:2])
    tau = step_ratio / omega
    sigma = step_ratio * omega

    def hours_of(r):
        return pl.ds(pl.multiple_of(r * hours, SUBLANES), hours)

    def over_regions(one):
        def several(i, _):
            first = i * pair
            together = pl.ds(pl.multiple_of(first * hours, 2 * SUBLANES), pair * hours)
            for chunk in chunks:
                bars = [one(first + j, chunk) for j in range(pair)]
                high, low = split_in_two(jnp.concatenate(bars, axis=0))
                bar_high[together, chunk] = high
                bar_low[together, chunk] = low
            return 0

        lax.fori_loop(0, regions // pair, several, 0)

    def keep_sums(r, chunk, bar):
        year_sum[pl.ds(r, 1), chunk] = jnp.sum(bar, axis=0, keepdims=True)
        if chunk.start < units:
            charge[hours_of(r), :] = bar[:, :units]

    def first_primal(r, chunk):
        c = cost[r, :, chunk].astype(f32)
        low, high = lower[pl.ds(r, 1), chunk], upper[pl.ds(r, 1), chunk]
        return c, low, high, jnp.clip(-tau * c, low, high)

    def first_pass(r, chunk):
        bar = 2.0 * first_primal(r, chunk)[3]
        keep_sums(r, chunk, bar)
        return bar

    over_regions(first_pass)

    def send_sums(phase, send, recv):
        def run_levels(t, level):
            level = keep[t] * level + charge[pl.ds(t, regions, stride=hours), :]
            levels[t] = level
            return level

        level = padded(lax.fori_loop(0, hours, run_levels, zero_units, unroll=4), rows)
        for owner in range(time_count):
            send[owner, 0:rows, :] = level
            for j in range(share):
                tile = owner * share + j
                if tile < tiles:
                    half, block = tile // blocks, tile % blocks
                    part = year_sum[
                        half * SUBLANES : (half + 1) * SUBLANES,
                        block * LANES : (block + 1) * LANES,
                    ]
                else:
                    part = jnp.zeros((SUBLANES, LANES), f32)
                at = rows + j * SUBLANES
                send[owner, at : at + SUBLANES, :] = part
        recv[me] = send[me]
        send_time(phase, lambda peer: send.at[peer], recv)

    def matmul_image():
        image[...] = product(bar_high[...], bar_low[...], conv_high[...], conv_low[...], 0)

    send_sums(1, spread_send, spread_recv)
    matmul_image()

    def first_prices(i, bus):
        first = i * pair
        together = pl.ds(pl.multiple_of(first * hours, 2 * SUBLANES), pair * hours)
        parts = []
        for j in range(pair):
            r = first + j
            p = sigma * (image[hours_of(r), :] - demand[r].astype(f32))
            prices[hours_of(r), :] = p
            bus = jnp.where(spot == r, p[:, 0:1], bus)
            parts.append(p)
        high, low = split_in_two(jnp.concatenate(parts, axis=0))
        price_high[together, :] = high
        price_low[together, :] = low
        return bus

    bus_recv[group] = lax.fori_loop(
        0, regions // pair, first_prices, jnp.zeros((hours, bus_width), f32)
    )
    send_group(1, bus_recv)
    back[...] = product(price_high[...], price_low[...], conv_high[...], conv_low[...], 1)

    await_bytes(spread_recv, time_count, recv_sem.at[1])

    def carried(recv):
        def one(j, state):
            return first_recv[j, 0:rows, :] * state + recv[j, 0:rows, :]

        state = lax.fori_loop(0, me, one, jnp.zeros((rows, units), f32))
        return state[0:regions]

    def year_total(recv):
        return jnp.sum(recv[:, rows:, :], axis=0)

    own_year = year_total(spread_recv)
    turn = carried(spread_recv)
    caps = energy_cap[...]

    def first_storage(t, run):
        run = keep[t] * run
        dual = jnp.maximum(sigma * (scale * (levels[t] + run) - caps), 0.0)
        storage[t] = dual
        return run

    lax.fori_loop(0, hours, first_storage, turn, unroll=4)

    def adjoint_only(i, run):
        t = hours - 1 - i
        return keep[t] * (scale * storage[t] + run)

    run = lax.fori_loop(0, hours, adjoint_only, zero_units, unroll=4)
    turn_send[0:rows, :] = padded(run, rows)
    turn_send[rows:, :] = own_year
    turn_recv[me, 0:rows, :] = padded(run, rows)
    turn_recv[me, rows:, :] = own_year
    send_time(2, lambda peer: turn_send, turn_recv)

    await_bytes(bus_recv, group_count, group_recv_sem.at[1])
    exact = functools.partial(
        lax.dot_general, precision=lax.Precision.HIGHEST, preferred_element_type=f32
    )
    bus = jnp.sum(bus_recv[...], axis=0)
    flow_grad = exact(bus, incidence, (((1,), (0,)), ((), ())))
    caps_of_lines = line_cap[...]
    flows = jnp.clip(-tau * flow_grad, -caps_of_lines, caps_of_lines)
    flows_out[...] = flows
    inflow_recv[group] = exact(2.0 * flows, incidence, (((1,), (1,)), ((), ())))
    send_group(2, inflow_recv)

    await_bytes(turn_recv, time_count, recv_sem.at[2])

    def ahead(i, state):
        j = time_count - 1 - i
        return first_recv[j, 0:rows, :] * state + turn_recv[j, 0:rows, :]

    run = lax.fori_loop(0, time_count - 1 - me, ahead, jnp.zeros((rows, units), f32))[0:regions]

    def adjoint(i, run):
        t = hours - 1 - i
        value = scale * storage[t] + run
        stored[pl.ds(t, regions, stride=hours), :] = value
        return keep[t] * value

    lax.fori_loop(0, hours, adjoint, run, unroll=4)

    def year_parts(recv_tile):
        for tile in range(tiles):
            half, block = tile // blocks, tile % blocks
            first = half * SUBLANES
            last = min(first + SUBLANES, regions)
            if last <= first:
                continue
            at = rows + (tile % share) * SUBLANES
            total = recv_tile(tile // share, at)[0 : last - first]
            cap = annual_cap[first:last, block * LANES : (block + 1) * LANES]
            step = sigma * (scale * total - year_bound * cap)
            yield slice(first, last), slice(block * LANES, (block + 1) * LANES), step

    for r, c, step in year_parts(lambda owner, at: turn_recv[owner, at : at + SUBLANES, :]):
        year_dual[r, c] = jnp.maximum(step, 0.0)

    def second_pass(r, chunk):
        c, low, high, x = first_primal(r, chunk)
        grad = c + back[hours_of(r), chunk] + scale * year_dual[pl.ds(r, 1), chunk]
        if chunk.start < units:
            grad = jnp.concatenate(
                [grad[:, :units] + stored[hours_of(r), :], grad[:, units:]], axis=1
            )
        new = jnp.clip(x - tau * grad, low, high)
        primal_out[r, :, chunk] = new.astype(jnp.bfloat16)
        bar = 2.0 * new - x
        keep_sums(r, chunk, bar)
        return bar

    over_regions(second_pass)
    send_sums(3, again_send, again_recv)
    matmul_image()
    await_bytes(inflow_recv, group_count, group_recv_sem.at[2])
    inflow = jnp.sum(inflow_recv[...], axis=0)
    bus_row = lax.broadcasted_iota(jnp.int32, (hours, rows_bus), 1) == 0

    def second_prices(r, _):
        load = demand[r].astype(f32)
        into = jnp.sum(jnp.where(spot == r, inflow, 0.0), axis=1, keepdims=True)
        whole = image[hours_of(r), :] + jnp.where(bus_row, into, 0.0)
        prices_out[r] = prices[hours_of(r), :] + sigma * (whole - load)
        return 0

    lax.fori_loop(0, regions, second_prices, 0)

    await_bytes(again_recv, time_count, recv_sem.at[3])
    own_year = year_total(again_recv)
    last_send[...] = own_year
    last_recv[me] = own_year
    send_time(4, lambda peer: last_send, last_recv)
    turn = carried(again_recv)

    def second_storage(t, run):
        run = keep[t] * run
        storage_out[pl.ds(t, regions, stride=hours), :] = jnp.maximum(
            storage[t] + sigma * (scale * (levels[t] + run) - caps), 0.0
        )
        return run

    lax.fori_loop(0, hours, second_storage, turn, unroll=4)
    await_bytes(last_recv, time_count, recv_sem.at[4])
    for r, c, step in year_parts(
        lambda owner, at: last_recv[owner, at - rows : at - rows + SUBLANES, :]
    ):
        year_out[r, c] = jnp.maximum(year_dual[r, c] + step, 0.0)

    for phase, recv in enumerate((first_recv, spread_recv, turn_recv, again_recv, last_recv)):
        await_bytes(recv, time_count, send_sem.at[phase])
    for phase, recv in enumerate((square_recv, bus_recv, inflow_recv)):
        await_bytes(recv, group_count, group_send_sem.at[phase])


def deliver(*refs):
    count = (len(refs) - 1) // 2
    sem = refs[-1]
    copies = [
        pltpu.make_async_copy(refs[i], refs[count + i], sem.at[i]) for i in range(count)
    ]
    for copy in copies:
        copy.start()
    for copy in copies:
        copy.wait()


def delivered(arrays):
    return pl.pallas_call(
        deliver,
        out_shape=tuple(jax.ShapeDtypeStruct(a.shape, a.dtype) for a in arrays),
        in_specs=[pl.BlockSpec(memory_space=pltpu.VMEM)] * len(arrays),
        out_specs=[pl.BlockSpec(memory_space=pl.ANY)] * len(arrays),
        scratch_shapes=[pltpu.SemaphoreType.DMA((len(arrays),))],
        compiler_params=pltpu.CompilerParams(vmem_limit_bytes=8 * 2**20),
    )(*arrays)


def per_device(
    time_count,
    group_count,
    cost,
    demand,
    conversion,
    upper,
    decay,
    energy_cap,
    annual_cap,
    line_ends,
    line_cap,
):
    f32, bf16 = jnp.float32, jnp.bfloat16
    hours, regions, width = cost.shape
    rows_bus = demand.shape[2]
    units = decay.shape[2]
    lines = line_ends.shape[0]
    rows = up_to(regions, 2 * SUBLANES)
    bus_width = up_to(regions * group_count, LANES)
    tiles = (rows // SUBLANES) * (width // LANES)
    share = -(-tiles // time_count) * SUBLANES
    vmem = pl.BlockSpec(memory_space=pltpu.VMEM)
    scratch = lambda *shape: pltpu.VMEM(shape, f32)
    half = lambda *shape: pltpu.VMEM(shape, bf16)
    flat = hours * regions
    by_region = lambda x: jnp.transpose(x, (1, 0, 2))
    results = pl.pallas_call(
        functools.partial(kernel, time_count, group_count),
        out_shape=(
            jax.ShapeDtypeStruct((regions, hours, width), bf16),
            jax.ShapeDtypeStruct((hours, lines), f32),
            jax.ShapeDtypeStruct((regions, hours, rows_bus), f32),
            jax.ShapeDtypeStruct((flat, units), f32),
            jax.ShapeDtypeStruct((regions, width), f32),
        ),
        in_specs=[vmem] * 9,
        out_specs=[vmem] * 5,
        scratch_shapes=[
            half(width, rows_bus),
            half(width, rows_bus),
            half(flat, width),
            half(flat, width),
            half(flat, rows_bus),
            half(flat, rows_bus),
            scratch(flat, rows_bus),
            scratch(flat, rows_bus),
            scratch(flat, width),
            scratch(hours, regions, units),
            scratch(flat, units),
            scratch(hours, regions, units),
            scratch(hours, regions, units),
            scratch(flat, units),
            scratch(rows, width),
            scratch(rows, width),
            scratch(rows, width),
            scratch(group_count, SUBLANES, LANES),
            scratch(group_count, hours, bus_width),
            scratch(group_count, hours, bus_width),
            scratch(rows + SUBLANES, units),
            scratch(time_count, rows + SUBLANES, units),
            scratch(time_count, rows + share, units),
            scratch(time_count, rows + share, units),
            scratch(rows + share, units),
            scratch(time_count, rows + share, units),
            scratch(time_count, rows + share, units),
            scratch(time_count, rows + share, units),
            scratch(share, units),
            scratch(time_count, share, units),
            pltpu.SemaphoreType.DMA((5,)),
            pltpu.SemaphoreType.DMA((5,)),
            pltpu.SemaphoreType.DMA((3,)),
            pltpu.SemaphoreType.DMA((3,)),
        ],
        compiler_params=pltpu.CompilerParams(
            collective_id=0, has_side_effects=True, vmem_limit_bytes=20 * 2**20
        ),
    )(
        by_region(cost),
        by_region(demand),
        conversion,
        upper,
        by_region(decay).reshape(flat, units),
        energy_cap,
        annual_cap,
        line_ends.T,
        line_cap.reshape(1, lines),
    )
    primal, flows, prices, storage, year = delivered(results)
    return (
        by_region(primal),
        flows,
        by_region(prices),
        by_region(storage.reshape(regions, hours, units)),
        year,
    )


def solution(mesh):
    in_specs = (
        P("tm", "region", None),
        P("tm", "region", None),
        P(),
        P("region", None),
        P("tm", "region", None),
        P("region", None),
        P("region", None),
        P("region", None),
        P("region"),
    )
    out_specs = (
        P("tm", "region", None),
        P("tm", "region"),
        P("tm", "region", None),
        P("tm", "region", None),
        P("region", None),
    )
    return jax.shard_map(
        functools.partial(per_device, mesh.shape["tm"], mesh.shape["region"]),
        mesh=mesh,
        in_specs=in_specs,
        out_specs=out_specs,
        check_vma=False,
    )
```

```python
import functools
import math

import jax
import jax.numpy as jnp
from jax import lax
from jax.experimental import pallas as pl
from jax.experimental.pallas import tpu as pltpu
from jax.sharding import PartitionSpec as P

step_ratio = 0.5
LANES = 128
SUBLANES = 8
CHUNK = 256


def up_to(value, multiple):
    return -(-value // multiple) * multiple


def padded(x, rows):
    missing = rows - x.shape[0]
    if missing == 0:
        return x
    return jnp.concatenate([x, jnp.zeros((missing,) + x.shape[1:], x.dtype)], axis=0)


def split_in_two(x):
    high = x.astype(jnp.bfloat16)
    return high, (x - high.astype(jnp.float32)).astype(jnp.bfloat16)


def product(a_high, a_low, b_high, b_low, contract_b):
    dims = (((1,), (contract_b,)), ((), ()))
    dot = functools.partial(
        lax.dot_general, dimension_numbers=dims, preferred_element_type=jnp.float32
    )
    return dot(a_high, b_high) + (dot(a_high, b_low) + dot(a_low, b_high))


def kernel(
    time_count,
    group_count,
    cost_far,
    demand_far,
    conversion_far,
    upper_far,
    decay_far,
    energy_cap_far,
    annual_cap_far,
    line_ends_far,
    line_cap_far,
    primal_out,
    flows_out,
    prices_out,
    storage_out,
    year_out,
    cost,
    demand,
    conversion,
    upper,
    decay,
    energy_cap,
    annual_cap,
    line_ends,
    line_cap,
    conv_high,
    conv_low,
    bar_high,
    bar_low,
    price_high,
    price_low,
    prices,
    image,
    back,
    keep,
    charge,
    levels,
    storage,
    stored,
    lower,
    year_sum,
    year_dual,
    square_recv,
    bus_recv,
    inflow_recv,
    first_send,
    first_recv,
    carry_send,
    carry_recv,
    part_send,
    part_recv,
    whole_send,
    whole_recv,
    send_sem,
    recv_sem,
    group_send_sem,
    group_recv_sem,
    load_sem,
):
    me = lax.axis_index("tm")
    group = lax.axis_index("region")
    regions, hours, width = cost.shape
    rows_bus = demand.shape[2]
    units = decay.shape[1]
    rows = lower.shape[0]
    pair = (2 * SUBLANES) // math.gcd(hours, 2 * SUBLANES)
    chunks = [slice(i, i + CHUNK) for i in range(0, width, CHUNK)]
    blocks = width // LANES
    tiles = (rows // SUBLANES) * blocks
    share = -(-tiles // time_count)
    hours_all = hours * time_count
    scale = 1.0 / math.sqrt(hours_all)
    year_bound = math.sqrt(hours_all)
    f32 = jnp.float32

    loads = {}
    for i, (name, far, near) in enumerate(
        (
            ("cost", cost_far, cost),
            ("demand", demand_far, demand),
            ("decay", decay_far, decay),
            ("upper", upper_far, upper),
            ("conversion", conversion_far, conversion),
            ("energy_cap", energy_cap_far, energy_cap),
            ("annual_cap", annual_cap_far, annual_cap),
            ("line_ends", line_ends_far, line_ends),
            ("line_cap", line_cap_far, line_cap),
        )
    ):
        loads[name] = pltpu.make_async_copy(far, near, load_sem.at[i])
        loads[name].start()

    barrier = pltpu.get_barrier_semaphore()

    def greet_time(k, _):
        pl.semaphore_signal(
            barrier,
            inc=1,
            device_id={"tm": lax.rem(me + k, time_count)},
            device_id_type=pl.DeviceIdType.MESH,
        )
        return 0

    lax.fori_loop(1, time_count, greet_time, 0)

    def greet_group(k, _):
        pl.semaphore_signal(
            barrier,
            inc=1,
            device_id={"region": lax.rem(group + k, group_count)},
            device_id_type=pl.DeviceIdType.MESH,
        )
        return 0

    lax.fori_loop(1, group_count, greet_group, 0)

    def send_time(phase, source_of, recv):
        def one(k, _):
            peer = lax.rem(me + k, time_count)
            pltpu.make_async_remote_copy(
                src_ref=source_of(peer),
                dst_ref=recv.at[me],
                send_sem=send_sem.at[phase],
                recv_sem=recv_sem.at[phase],
                device_id={"tm": peer},
                device_id_type=pl.DeviceIdType.MESH,
            ).start()
            return 0

        lax.fori_loop(1, time_count, one, 0)

    def send_group(phase, recv):
        def one(k, _):
            pltpu.make_async_remote_copy(
                src_ref=recv.at[group],
                dst_ref=recv.at[group],
                send_sem=group_send_sem.at[phase],
                recv_sem=group_recv_sem.at[phase],
                device_id={"region": lax.rem(group + k, group_count)},
                device_id_type=pl.DeviceIdType.MESH,
            ).start()
            return 0

        lax.fori_loop(1, group_count, one, 0)

    def await_bytes(recv, count, sem):
        if count > 1:
            part = recv.at[pl.ds(0, count - 1)]
            pltpu.make_async_copy(part, part, sem).wait()

    loads["cost"].wait()
    loads["demand"].wait()
    def square_sums(r, carry):
        a, b = carry
        for chunk in chunks:
            c = cost[r, :, chunk].astype(f32)
            a = a + c * c
        l = demand[r].astype(f32)
        return a, b + l * l

    a, b = lax.fori_loop(
        0,
        regions,
        square_sums,
        (jnp.zeros((hours, CHUNK), f32), jnp.zeros((hours, rows_bus), f32)),
    )
    loads["decay"].wait()
    zero_units = jnp.zeros((regions, units), f32)
    for t in range(hours):
        keep[t] = decay[pl.ds(t, regions, stride=hours), :]

    whole_decay = lax.fori_loop(
        0, hours, lambda t, d: d * keep[t], jnp.ones((regions, units), f32)
    )

    def folded(x):
        x = jnp.sum(x, axis=0, keepdims=True)
        return sum(x[:, i * LANES : (i + 1) * LANES] for i in range(x.shape[1] // LANES))

    own_squares = padded(jnp.concatenate([folded(a), folded(b)], axis=0), SUBLANES)
    square_recv[group] = own_squares
    pl.semaphore_wait(barrier, time_count - 1 + group_count - 1)
    send_group(0, square_recv)
    await_bytes(square_recv, group_count, group_recv_sem.at[0])
    squares = jnp.sum(square_recv[...], axis=0)
    first_send[0:rows, :] = padded(whole_decay, rows)
    first_send[rows : rows + SUBLANES, :] = squares
    first_recv[me, 0:rows, :] = padded(whole_decay, rows)
    first_recv[me, rows : rows + SUBLANES, :] = squares
    send_time(0, lambda peer: first_send, first_recv)

    for name in ("upper", "conversion", "energy_cap", "annual_cap", "line_ends", "line_cap"):
        loads[name].wait()
    column = lax.broadcasted_iota(jnp.int32, (regions, width), 1)
    lower[0:regions, :] = jnp.where(column < units, -upper[...], 0.0)
    year_sum[...] = jnp.zeros_like(year_sum)
    conv = conversion[...]
    high, low = split_in_two(conv)
    conv_high[...] = high
    conv_low[...] = low

    bus_width = bus_recv.shape[2]
    ends = line_ends[...]
    region_id = lax.broadcasted_iota(jnp.int32, (bus_width, ends.shape[1]), 0)
    incidence = (ends[1:2, :] == region_id).astype(f32) - (ends[0:1, :] == region_id).astype(f32)
    spot = lax.broadcasted_iota(jnp.int32, (hours, bus_width), 1) - group * regions

    await_bytes(first_recv, time_count, recv_sem.at[0])
    squares = jnp.sum(first_recv[:, rows : rows + SUBLANES, :], axis=0)
    sums = jnp.sum(squares, axis=1, keepdims=True)
    omega = jnp.sqrt(sums[0:1] / sums[1:2])
    tau = step_ratio / omega
    sigma = step_ratio * omega

    def hours_of(r):
        return pl.ds(pl.multiple_of(r * hours, SUBLANES), hours)

    def over_regions(one):
        def several(i, _):
            first = i * pair
            together = pl.ds(pl.multiple_of(first * hours, 2 * SUBLANES), pair * hours)
            for chunk in chunks:
                bars = [one(first + j, chunk) for j in range(pair)]
                high, low = split_in_two(jnp.concatenate(bars, axis=0))
                bar_high[together, chunk] = high
                bar_low[together, chunk] = low
            return 0

        lax.fori_loop(0, regions // pair, several, 0)

    def keep_sums(r, chunk, bar):
        year_sum[pl.ds(r, 1), chunk] = jnp.sum(bar, axis=0, keepdims=True)
        if chunk.start < units:
            charge[hours_of(r), :] = bar[:, :units]

    def first_primal(r, chunk):
        c = cost[r, :, chunk].astype(f32)
        low, high = lower[pl.ds(r, 1), chunk], upper[pl.ds(r, 1), chunk]
        return c, low, high, jnp.clip(-tau * c, low, high)

    def first_pass(r, chunk):
        bar = 2.0 * first_primal(r, chunk)[3]
        keep_sums(r, chunk, bar)
        return bar

    over_regions(first_pass)

    def send_carry(phase, at, value):
        carry_send[at] = padded(value, rows)
        carry_recv[at, me] = padded(value, rows)
        send_time(phase, lambda peer: carry_send.at[at], carry_recv.at[at])

    def send_levels(phase, at):
        def run_levels(t, level):
            level = keep[t] * level + charge[pl.ds(t, regions, stride=hours), :]
            levels[t] = level
            return level

        send_carry(phase, at, lax.fori_loop(0, hours, run_levels, zero_units, unroll=4))

    def send_parts(phase, at):
        for owner in range(time_count):
            for j in range(share):
                tile = owner * share + j
                if tile < tiles:
                    half, block = tile // blocks, tile % blocks
                    part = year_sum[
                        half * SUBLANES : (half + 1) * SUBLANES,
                        block * LANES : (block + 1) * LANES,
                    ]
                else:
                    part = jnp.zeros((SUBLANES, LANES), f32)
                part_send[at, owner, j * SUBLANES : (j + 1) * SUBLANES, :] = part
        part_recv[at, me] = part_send[at, me]
        send_time(phase, lambda peer: part_send.at[at, peer], part_recv.at[at])

    def send_whole(phase, at):
        own = jnp.sum(part_recv[at], axis=0)
        whole_send[at] = own
        whole_recv[at, me] = own
        send_time(phase, lambda peer: whole_send.at[at], whole_recv.at[at])

    def matmul_image():
        image[...] = product(bar_high[...], bar_low[...], conv_high[...], conv_low[...], 0)

    send_levels(1, 0)
    send_parts(2, 0)
    matmul_image()

    def first_prices(i, bus):
        first = i * pair
        together = pl.ds(pl.multiple_of(first * hours, 2 * SUBLANES), pair * hours)
        parts = []
        for j in range(pair):
            r = first + j
            p = sigma * (image[hours_of(r), :] - demand[r].astype(f32))
            prices[hours_of(r), :] = p
            bus = jnp.where(spot == r, p[:, 0:1], bus)
            parts.append(p)
        high, low = split_in_two(jnp.concatenate(parts, axis=0))
        price_high[together, :] = high
        price_low[together, :] = low
        return bus

    bus_recv[group] = lax.fori_loop(
        0, regions // pair, first_prices, jnp.zeros((hours, bus_width), f32)
    )
    send_group(1, bus_recv)
    back[...] = product(price_high[...], price_low[...], conv_high[...], conv_low[...], 1)

    await_bytes(carry_recv.at[0], time_count, recv_sem.at[1])

    def carried(at):
        def one(j, state):
            return first_recv[j, 0:rows, :] * state + carry_recv[at, j]

        state = lax.fori_loop(0, me, one, jnp.zeros((rows, units), f32))
        return state[0:regions]

    turn = carried(0)
    caps = energy_cap[...]

    def first_storage(t, run):
        run = keep[t] * run
        dual = jnp.maximum(sigma * (scale * (levels[t] + run) - caps), 0.0)
        storage[t] = dual
        return run

    lax.fori_loop(0, hours, first_storage, turn, unroll=4)

    def adjoint_only(i, run):
        t = hours - 1 - i
        return keep[t] * (scale * storage[t] + run)

    run = lax.fori_loop(0, hours, adjoint_only, zero_units, unroll=4)
    send_carry(3, 1, run)
    await_bytes(part_recv.at[0], time_count, recv_sem.at[2])
    send_whole(4, 0)

    await_bytes(bus_recv, group_count, group_recv_sem.at[1])
    exact = functools.partial(
        lax.dot_general, precision=lax.Precision.HIGHEST, preferred_element_type=f32
    )
    bus = jnp.sum(bus_recv[...], axis=0)
    flow_grad = exact(bus, incidence, (((1,), (0,)), ((), ())))
    caps_of_lines = line_cap[...]
    flows = jnp.clip(-tau * flow_grad, -caps_of_lines, caps_of_lines)
    flows_out[...] = flows
    inflow_recv[group] = exact(2.0 * flows, incidence, (((1,), (1,)), ((), ())))
    send_group(2, inflow_recv)

    await_bytes(carry_recv.at[1], time_count, recv_sem.at[3])

    def ahead(i, state):
        j = time_count - 1 - i
        return first_recv[j, 0:rows, :] * state + carry_recv[1, j]

    run = lax.fori_loop(0, time_count - 1 - me, ahead, jnp.zeros((rows, units), f32))[0:regions]

    def adjoint(i, run):
        t = hours - 1 - i
        value = scale * storage[t] + run
        stored[pl.ds(t, regions, stride=hours), :] = value
        return keep[t] * value

    lax.fori_loop(0, hours, adjoint, run, unroll=4)

    def year_parts(at):
        for tile in range(tiles):
            half, block = tile // blocks, tile % blocks
            first = half * SUBLANES
            last = min(first + SUBLANES, regions)
            if last <= first:
                continue
            down = (tile % share) * SUBLANES
            total = whole_recv[at, tile // share, down : down + last - first, :]
            cap = annual_cap[first:last, block * LANES : (block + 1) * LANES]
            step = sigma * (scale * total - year_bound * cap)
            yield slice(first, last), slice(block * LANES, (block + 1) * LANES), step

    await_bytes(whole_recv.at[0], time_count, recv_sem.at[4])
    for r, c, step in year_parts(0):
        year_dual[r, c] = jnp.maximum(step, 0.0)

    def second_pass(r, chunk):
        c, low, high, x = first_primal(r, chunk)
        grad = c + back[hours_of(r), chunk] + scale * year_dual[pl.ds(r, 1), chunk]
        if chunk.start < units:
            grad = jnp.concatenate(
                [grad[:, :units] + stored[hours_of(r), :], grad[:, units:]], axis=1
            )
        new = jnp.clip(x - tau * grad, low, high)
        primal_out[r, :, chunk] = new.astype(jnp.bfloat16)
        bar = 2.0 * new - x
        keep_sums(r, chunk, bar)
        return bar

    over_regions(second_pass)
    send_parts(5, 1)
    send_levels(6, 2)
    matmul_image()
    await_bytes(inflow_recv, group_count, group_recv_sem.at[2])
    inflow = jnp.sum(inflow_recv[...], axis=0)
    bus_row = lax.broadcasted_iota(jnp.int32, (hours, rows_bus), 1) == 0

    def second_prices(r, _):
        load = demand[r].astype(f32)
        into = jnp.sum(jnp.where(spot == r, inflow, 0.0), axis=1, keepdims=True)
        whole = image[hours_of(r), :] + jnp.where(bus_row, into, 0.0)
        prices_out[r] = prices[hours_of(r), :] + sigma * (whole - load)
        return 0

    lax.fori_loop(0, regions, second_prices, 0)

    await_bytes(part_recv.at[1], time_count, recv_sem.at[5])
    send_whole(7, 1)
    await_bytes(carry_recv.at[2], time_count, recv_sem.at[6])
    turn = carried(2)

    def second_storage(t, run):
        run = keep[t] * run
        storage_out[pl.ds(t, regions, stride=hours), :] = jnp.maximum(
            storage[t] + sigma * (scale * (levels[t] + run) - caps), 0.0
        )
        return run

    lax.fori_loop(0, hours, second_storage, turn, unroll=4)
    await_bytes(whole_recv.at[1], time_count, recv_sem.at[7])
    for r, c, step in year_parts(1):
        year_out[r, c] = jnp.maximum(year_dual[r, c] + step, 0.0)

    sent = (
        first_recv,
        carry_recv.at[0],
        part_recv.at[0],
        carry_recv.at[1],
        whole_recv.at[0],
        part_recv.at[1],
        carry_recv.at[2],
        whole_recv.at[1],
    )
    for phase, recv in enumerate(sent):
        await_bytes(recv, time_count, send_sem.at[phase])
    for phase, recv in enumerate((square_recv, bus_recv, inflow_recv)):
        await_bytes(recv, group_count, group_send_sem.at[phase])


def deliver(*refs):
    count = (len(refs) - 1) // 2
    sem = refs[-1]
    copies = [
        pltpu.make_async_copy(refs[i], refs[count + i], sem.at[i]) for i in range(count)
    ]
    for copy in copies:
        copy.start()
    for copy in copies:
        copy.wait()


def delivered(arrays):
    return pl.pallas_call(
        deliver,
        out_shape=tuple(jax.ShapeDtypeStruct(a.shape, a.dtype) for a in arrays),
        in_specs=[pl.BlockSpec(memory_space=pltpu.VMEM)] * len(arrays),
        out_specs=[pl.BlockSpec(memory_space=pl.ANY)] * len(arrays),
        scratch_shapes=[pltpu.SemaphoreType.DMA((len(arrays),))],
        compiler_params=pltpu.CompilerParams(vmem_limit_bytes=8 * 2**20),
    )(*arrays)


def per_device(
    time_count,
    group_count,
    cost,
    demand,
    conversion,
    upper,
    decay,
    energy_cap,
    annual_cap,
    line_ends,
    line_cap,
):
    f32, bf16 = jnp.float32, jnp.bfloat16
    hours, regions, width = cost.shape
    rows_bus = demand.shape[2]
    units = decay.shape[2]
    lines = line_ends.shape[0]
    rows = up_to(regions, 2 * SUBLANES)
    bus_width = up_to(regions * group_count, LANES)
    tiles = (rows // SUBLANES) * (width // LANES)
    share = -(-tiles // time_count) * SUBLANES
    vmem = pl.BlockSpec(memory_space=pltpu.VMEM)
    scratch = lambda *shape: pltpu.VMEM(shape, f32)
    half = lambda *shape: pltpu.VMEM(shape, bf16)
    flat = hours * regions
    by_region = lambda x: jnp.transpose(x, (1, 0, 2))
    operands = (
        by_region(cost),
        by_region(demand),
        conversion,
        upper,
        by_region(decay).reshape(flat, units),
        energy_cap,
        annual_cap,
        line_ends.T,
        line_cap.reshape(1, lines),
    )
    operands = tuple(pltpu.with_memory_space_constraint(x, pltpu.HBM) for x in operands)
    results = pl.pallas_call(
        functools.partial(kernel, time_count, group_count),
        out_shape=(
            jax.ShapeDtypeStruct((regions, hours, width), bf16),
            jax.ShapeDtypeStruct((hours, lines), f32),
            jax.ShapeDtypeStruct((regions, hours, rows_bus), f32),
            jax.ShapeDtypeStruct((flat, units), f32),
            jax.ShapeDtypeStruct((regions, width), f32),
        ),
        in_specs=[pl.BlockSpec(memory_space=pltpu.HBM)] * len(operands),
        out_specs=[vmem] * 5,
        scratch_shapes=[pltpu.VMEM(x.shape, x.dtype) for x in operands]
        + [
            half(width, rows_bus),
            half(width, rows_bus),
            half(flat, width),
            half(flat, width),
            half(flat, rows_bus),
            half(flat, rows_bus),
            scratch(flat, rows_bus),
            scratch(flat, rows_bus),
            scratch(flat, width),
            scratch(hours, regions, units),
            scratch(flat, units),
            scratch(hours, regions, units),
            scratch(hours, regions, units),
            scratch(flat, units),
            scratch(rows, width),
            scratch(rows, width),
            scratch(rows, width),
            scratch(group_count, SUBLANES, LANES),
            scratch(group_count, hours, bus_width),
            scratch(group_count, hours, bus_width),
            scratch(rows + SUBLANES, units),
            scratch(time_count, rows + SUBLANES, units),
            scratch(3, rows, units),
            scratch(3, time_count, rows, units),
            scratch(2, time_count, share, LANES),
            scratch(2, time_count, share, LANES),
            scratch(2, share, LANES),
            scratch(2, time_count, share, LANES),
            pltpu.SemaphoreType.DMA((8,)),
            pltpu.SemaphoreType.DMA((8,)),
            pltpu.SemaphoreType.DMA((3,)),
            pltpu.SemaphoreType.DMA((3,)),
            pltpu.SemaphoreType.DMA((9,)),
        ],
        compiler_params=pltpu.CompilerParams(
            collective_id=0, has_side_effects=True, vmem_limit_bytes=20 * 2**20
        ),
    )(*operands)
    primal, flows, prices, storage, year = delivered(results)
    return (
        by_region(primal),
        flows,
        by_region(prices),
        by_region(storage.reshape(regions, hours, units)),
        year,
    )


def solution(mesh):
    in_specs = (
        P("tm", "region", None),
        P("tm", "region", None),
        P(),
        P("region", None),
        P("tm", "region", None),
        P("region", None),
        P("region", None),
        P("region", None),
        P("region"),
    )
    out_specs = (
        P("tm", "region", None),
        P("tm", "region"),
        P("tm", "region", None),
        P("tm", "region", None),
        P("region", None),
    )
    return jax.shard_map(
        functools.partial(per_device, mesh.shape["tm"], mesh.shape["region"]),
        mesh=mesh,
        in_specs=in_specs,
        out_specs=out_specs,
        check_vma=False,
    )
```

```python
import functools
import math

import jax
import jax.numpy as jnp
from jax import lax
from jax.experimental import pallas as pl
from jax.experimental.pallas import tpu as pltpu
from jax.sharding import PartitionSpec as P

step_ratio = 0.5
LANES = 128
SUBLANES = 8
CHUNK = 256


def up_to(value, multiple):
    return -(-value // multiple) * multiple


def padded(x, rows):
    missing = rows - x.shape[0]
    if missing == 0:
        return x
    return jnp.concatenate([x, jnp.zeros((missing,) + x.shape[1:], x.dtype)], axis=0)


def split_in_two(x):
    high = x.astype(jnp.bfloat16)
    return high, (x - high.astype(jnp.float32)).astype(jnp.bfloat16)


def product(a_high, a_low, b_high, b_low, contract_b):
    dims = (((1,), (contract_b,)), ((), ()))
    dot = functools.partial(
        lax.dot_general, dimension_numbers=dims, preferred_element_type=jnp.float32
    )
    return dot(a_high, b_high) + (dot(a_high, b_low) + dot(a_low, b_high))


def kernel(
    time_count,
    group_count,
    cost_far,
    demand_far,
    conversion_far,
    upper_far,
    decay_far,
    energy_cap_far,
    annual_cap_far,
    line_ends_far,
    line_cap_far,
    primal_out,
    flows_out,
    prices_out,
    storage_out,
    year_out,
    cost,
    demand,
    conversion,
    upper,
    decay,
    energy_cap,
    annual_cap,
    line_ends,
    line_cap,
    conv_high,
    conv_low,
    bar_high,
    bar_low,
    price_high,
    price_low,
    prices,
    image,
    back,
    keep,
    charge,
    levels,
    storage,
    stored,
    lower,
    year_sum,
    year_dual,
    square_recv,
    bus_recv,
    inflow_recv,
    first_send,
    first_recv,
    carry_send,
    carry_recv,
    part_send,
    part_recv,
    whole_send,
    whole_recv,
    send_sem,
    recv_sem,
    group_send_sem,
    group_recv_sem,
    load_sem,
):
    me = lax.axis_index("tm")
    group = lax.axis_index("region")
    regions, hours, width = cost.shape
    rows_bus = demand.shape[2]
    units = decay.shape[1]
    rows = lower.shape[0]
    pair = (2 * SUBLANES) // math.gcd(hours, 2 * SUBLANES)
    chunks = [slice(i, i + CHUNK) for i in range(0, width, CHUNK)]
    blocks = width // LANES
    tiles = (rows // SUBLANES) * blocks
    share = -(-tiles // time_count)
    hours_all = hours * time_count
    scale = 1.0 / math.sqrt(hours_all)
    year_bound = math.sqrt(hours_all)
    f32 = jnp.float32

    loads = {}
    for i, (name, far, near) in enumerate(
        (
            ("cost", cost_far, cost),
            ("demand", demand_far, demand),
            ("decay", decay_far, decay),
            ("upper", upper_far, upper),
            ("conversion", conversion_far, conversion),
            ("energy_cap", energy_cap_far, energy_cap),
            ("annual_cap", annual_cap_far, annual_cap),
            ("line_ends", line_ends_far, line_ends),
            ("line_cap", line_cap_far, line_cap),
        )
    ):
        loads[name] = pltpu.make_async_copy(far, near, load_sem.at[i])
        loads[name].start()

    barrier = pltpu.get_barrier_semaphore()

    everyone = time_count * group_count
    mine = me * group_count + group

    def other(k):
        flat = lax.rem(mine + k, everyone)
        return {"tm": flat // group_count, "region": lax.rem(flat, group_count)}

    def greet(k, _):
        pl.semaphore_signal(
            barrier, inc=1, device_id=other(k), device_id_type=pl.DeviceIdType.MESH
        )
        return 0

    lax.fori_loop(1, everyone, greet, 0)

    def send_squares(k, _):
        pltpu.make_async_remote_copy(
            src_ref=square_recv.at[mine],
            dst_ref=square_recv.at[mine],
            send_sem=group_send_sem.at[0],
            recv_sem=group_recv_sem.at[0],
            device_id=other(k),
            device_id_type=pl.DeviceIdType.MESH,
        ).start()
        return 0

    def send_time(phase, source_of, recv):
        def one(k, _):
            peer = lax.rem(me + k, time_count)
            pltpu.make_async_remote_copy(
                src_ref=source_of(peer),
                dst_ref=recv.at[me],
                send_sem=send_sem.at[phase],
                recv_sem=recv_sem.at[phase],
                device_id={"tm": peer},
                device_id_type=pl.DeviceIdType.MESH,
            ).start()
            return 0

        lax.fori_loop(1, time_count, one, 0)

    def send_group(phase, recv):
        def one(k, _):
            pltpu.make_async_remote_copy(
                src_ref=recv.at[group],
                dst_ref=recv.at[group],
                send_sem=group_send_sem.at[phase],
                recv_sem=group_recv_sem.at[phase],
                device_id={"region": lax.rem(group + k, group_count)},
                device_id_type=pl.DeviceIdType.MESH,
            ).start()
            return 0

        lax.fori_loop(1, group_count, one, 0)

    def await_bytes(recv, count, sem):
        if count > 1:
            part = recv.at[pl.ds(0, count - 1)]
            pltpu.make_async_copy(part, part, sem).wait()

    loads["cost"].wait()
    loads["demand"].wait()
    def square_sums(r, carry):
        a, b = carry
        for chunk in chunks:
            c = cost[r, :, chunk].astype(f32)
            a = a + c * c
        l = demand[r].astype(f32)
        return a, b + l * l

    a, b = lax.fori_loop(
        0,
        regions,
        square_sums,
        (jnp.zeros((hours, CHUNK), f32), jnp.zeros((hours, rows_bus), f32)),
    )
    def total(x):
        return jnp.sum(jnp.sum(x, axis=0, keepdims=True), axis=1, keepdims=True)

    lane = lax.broadcasted_iota(jnp.int32, (1, LANES), 1)
    square_recv[mine] = jnp.where(lane == 0, total(a), total(b))
    pl.semaphore_wait(barrier, everyone - 1)
    lax.fori_loop(1, everyone, send_squares, 0)

    loads["decay"].wait()
    zero_units = jnp.zeros((regions, units), f32)
    for t in range(hours):
        keep[t] = decay[pl.ds(t, regions, stride=hours), :]

    whole_decay = lax.fori_loop(
        0, hours, lambda t, d: d * keep[t], jnp.ones((regions, units), f32)
    )

    first_send[...] = padded(whole_decay, rows)
    first_recv[me] = padded(whole_decay, rows)
    send_time(0, lambda peer: first_send, first_recv)

    for name in ("upper", "conversion", "energy_cap", "annual_cap", "line_ends", "line_cap"):
        loads[name].wait()
    column = lax.broadcasted_iota(jnp.int32, (regions, width), 1)
    lower[0:regions, :] = jnp.where(column < units, -upper[...], 0.0)
    year_sum[...] = jnp.zeros_like(year_sum)
    conv = conversion[...]
    high, low = split_in_two(conv)
    conv_high[...] = high
    conv_low[...] = low

    bus_width = bus_recv.shape[2]
    ends = line_ends[...]
    region_id = lax.broadcasted_iota(jnp.int32, (bus_width, ends.shape[1]), 0)
    incidence = (ends[1:2, :] == region_id).astype(f32) - (ends[0:1, :] == region_id).astype(f32)
    spot = lax.broadcasted_iota(jnp.int32, (hours, bus_width), 1) - group * regions

    await_bytes(square_recv, everyone, group_recv_sem.at[0])
    squares = jnp.sum(square_recv[...], axis=0)
    sums = squares[:, 0:1], squares[:, 1:2]
    omega = jnp.sqrt(sums[0] / sums[1])
    tau = step_ratio / omega
    sigma = step_ratio * omega

    def hours_of(r):
        return pl.ds(pl.multiple_of(r * hours, SUBLANES), hours)

    def over_regions(one):
        def several(i, _):
            first = i * pair
            together = pl.ds(pl.multiple_of(first * hours, 2 * SUBLANES), pair * hours)
            for chunk in chunks:
                bars = [one(first + j, chunk) for j in range(pair)]
                high, low = split_in_two(jnp.concatenate(bars, axis=0))
                bar_high[together, chunk] = high
                bar_low[together, chunk] = low
            return 0

        lax.fori_loop(0, regions // pair, several, 0)

    def keep_sums(r, chunk, bar):
        year_sum[pl.ds(r, 1), chunk] = jnp.sum(bar, axis=0, keepdims=True)
        if chunk.start < units:
            charge[hours_of(r), :] = bar[:, :units]

    def first_primal(r, chunk):
        c = cost[r, :, chunk].astype(f32)
        low, high = lower[pl.ds(r, 1), chunk], upper[pl.ds(r, 1), chunk]
        return c, low, high, jnp.clip(-tau * c, low, high)

    def first_pass(r, chunk):
        bar = 2.0 * first_primal(r, chunk)[3]
        keep_sums(r, chunk, bar)
        return bar

    over_regions(first_pass)

    def send_carry(phase, at, value):
        carry_send[at] = padded(value, rows)
        carry_recv[at, me] = padded(value, rows)
        send_time(phase, lambda peer: carry_send.at[at], carry_recv.at[at])

    def send_levels(phase, at):
        def run_levels(t, level):
            level = keep[t] * level + charge[pl.ds(t, regions, stride=hours), :]
            levels[t] = level
            return level

        send_carry(phase, at, lax.fori_loop(0, hours, run_levels, zero_units, unroll=4))

    def send_parts(phase, at):
        for owner in range(time_count):
            for j in range(share):
                tile = owner * share + j
                if tile < tiles:
                    half, block = tile // blocks, tile % blocks
                    part = year_sum[
                        half * SUBLANES : (half + 1) * SUBLANES,
                        block * LANES : (block + 1) * LANES,
                    ]
                else:
                    part = jnp.zeros((SUBLANES, LANES), f32)
                part_send[at, owner, j * SUBLANES : (j + 1) * SUBLANES, :] = part
        part_recv[at, me] = part_send[at, me]
        send_time(phase, lambda peer: part_send.at[at, peer], part_recv.at[at])

    def send_whole(phase, at):
        own = jnp.sum(part_recv[at], axis=0)
        whole_send[at] = own
        whole_recv[at, me] = own
        send_time(phase, lambda peer: whole_send.at[at], whole_recv.at[at])

    def matmul_image():
        image[...] = product(bar_high[...], bar_low[...], conv_high[...], conv_low[...], 0)

    send_levels(1, 0)
    send_parts(2, 0)
    matmul_image()

    def first_prices(i, bus):
        first = i * pair
        together = pl.ds(pl.multiple_of(first * hours, 2 * SUBLANES), pair * hours)
        parts = []
        for j in range(pair):
            r = first + j
            p = sigma * (image[hours_of(r), :] - demand[r].astype(f32))
            prices[hours_of(r), :] = p
            bus = jnp.where(spot == r, p[:, 0:1], bus)
            parts.append(p)
        high, low = split_in_two(jnp.concatenate(parts, axis=0))
        price_high[together, :] = high
        price_low[together, :] = low
        return bus

    bus_recv[group] = lax.fori_loop(
        0, regions // pair, first_prices, jnp.zeros((hours, bus_width), f32)
    )
    send_group(1, bus_recv)
    back[...] = product(price_high[...], price_low[...], conv_high[...], conv_low[...], 1)

    await_bytes(first_recv, time_count, recv_sem.at[0])
    await_bytes(carry_recv.at[0], time_count, recv_sem.at[1])

    def carried(at):
        def one(j, state):
            return first_recv[j] * state + carry_recv[at, j]

        state = lax.fori_loop(0, me, one, jnp.zeros((rows, units), f32))
        return state[0:regions]

    turn = carried(0)
    caps = energy_cap[...]

    def first_storage(t, run):
        run = keep[t] * run
        dual = jnp.maximum(sigma * (scale * (levels[t] + run) - caps), 0.0)
        storage[t] = dual
        return run

    lax.fori_loop(0, hours, first_storage, turn, unroll=4)

    def adjoint_only(i, run):
        t = hours - 1 - i
        return keep[t] * (scale * storage[t] + run)

    run = lax.fori_loop(0, hours, adjoint_only, zero_units, unroll=4)
    send_carry(3, 1, run)
    await_bytes(part_recv.at[0], time_count, recv_sem.at[2])
    send_whole(4, 0)

    await_bytes(bus_recv, group_count, group_recv_sem.at[1])
    exact = functools.partial(
        lax.dot_general, precision=lax.Precision.HIGHEST, preferred_element_type=f32
    )
    bus = jnp.sum(bus_recv[...], axis=0)
    flow_grad = exact(bus, incidence, (((1,), (0,)), ((), ())))
    caps_of_lines = line_cap[...]
    flows = jnp.clip(-tau * flow_grad, -caps_of_lines, caps_of_lines)
    flows_out[...] = flows
    inflow_recv[group] = exact(2.0 * flows, incidence, (((1,), (1,)), ((), ())))
    send_group(2, inflow_recv)

    await_bytes(carry_recv.at[1], time_count, recv_sem.at[3])

    def ahead(i, state):
        j = time_count - 1 - i
        return first_recv[j] * state + carry_recv[1, j]

    run = lax.fori_loop(0, time_count - 1 - me, ahead, jnp.zeros((rows, units), f32))[0:regions]

    def adjoint(i, run):
        t = hours - 1 - i
        value = scale * storage[t] + run
        stored[pl.ds(t, regions, stride=hours), :] = value
        return keep[t] * value

    lax.fori_loop(0, hours, adjoint, run, unroll=4)

    def year_parts(at):
        for tile in range(tiles):
            half, block = tile // blocks, tile % blocks
            first = half * SUBLANES
            last = min(first + SUBLANES, regions)
            if last <= first:
                continue
            down = (tile % share) * SUBLANES
            total = whole_recv[at, tile // share, down : down + last - first, :]
            cap = annual_cap[first:last, block * LANES : (block + 1) * LANES]
            step = sigma * (scale * total - year_bound * cap)
            yield slice(first, last), slice(block * LANES, (block + 1) * LANES), step

    await_bytes(whole_recv.at[0], time_count, recv_sem.at[4])
    for r, c, step in year_parts(0):
        year_dual[r, c] = jnp.maximum(step, 0.0)

    def second_pass(r, chunk):
        c, low, high, x = first_primal(r, chunk)
        grad = c + back[hours_of(r), chunk] + scale * year_dual[pl.ds(r, 1), chunk]
        if chunk.start < units:
            grad = jnp.concatenate(
                [grad[:, :units] + stored[hours_of(r), :], grad[:, units:]], axis=1
            )
        new = jnp.clip(x - tau * grad, low, high)
        primal_out[r, :, chunk] = new.astype(jnp.bfloat16)
        bar = 2.0 * new - x
        keep_sums(r, chunk, bar)
        return bar

    over_regions(second_pass)
    send_parts(5, 1)
    send_levels(6, 2)
    matmul_image()
    await_bytes(inflow_recv, group_count, group_recv_sem.at[2])
    inflow = jnp.sum(inflow_recv[...], axis=0)
    bus_row = lax.broadcasted_iota(jnp.int32, (hours, rows_bus), 1) == 0

    def second_prices(r, _):
        load = demand[r].astype(f32)
        into = jnp.sum(jnp.where(spot == r, inflow, 0.0), axis=1, keepdims=True)
        whole = image[hours_of(r), :] + jnp.where(bus_row, into, 0.0)
        prices_out[r] = prices[hours_of(r), :] + sigma * (whole - load)
        return 0

    lax.fori_loop(0, regions, second_prices, 0)

    await_bytes(part_recv.at[1], time_count, recv_sem.at[5])
    send_whole(7, 1)
    await_bytes(carry_recv.at[2], time_count, recv_sem.at[6])
    turn = carried(2)

    def second_storage(t, run):
        run = keep[t] * run
        storage_out[pl.ds(t, regions, stride=hours), :] = jnp.maximum(
            storage[t] + sigma * (scale * (levels[t] + run) - caps), 0.0
        )
        return run

    lax.fori_loop(0, hours, second_storage, turn, unroll=4)
    await_bytes(whole_recv.at[1], time_count, recv_sem.at[7])
    for r, c, step in year_parts(1):
        year_out[r, c] = jnp.maximum(year_dual[r, c] + step, 0.0)

    sent = (
        first_recv,
        carry_recv.at[0],
        part_recv.at[0],
        carry_recv.at[1],
        whole_recv.at[0],
        part_recv.at[1],
        carry_recv.at[2],
        whole_recv.at[1],
    )
    for phase, recv in enumerate(sent):
        await_bytes(recv, time_count, send_sem.at[phase])
    await_bytes(square_recv, everyone, group_send_sem.at[0])
    await_bytes(bus_recv, group_count, group_send_sem.at[1])
    await_bytes(inflow_recv, group_count, group_send_sem.at[2])


def deliver(*refs):
    count = (len(refs) - 1) // 2
    sem = refs[-1]
    copies = [
        pltpu.make_async_copy(refs[i], refs[count + i], sem.at[i]) for i in range(count)
    ]
    for copy in copies:
        copy.start()
    for copy in copies:
        copy.wait()


def delivered(arrays):
    return pl.pallas_call(
        deliver,
        out_shape=tuple(jax.ShapeDtypeStruct(a.shape, a.dtype) for a in arrays),
        in_specs=[pl.BlockSpec(memory_space=pltpu.VMEM)] * len(arrays),
        out_specs=[pl.BlockSpec(memory_space=pl.ANY)] * len(arrays),
        scratch_shapes=[pltpu.SemaphoreType.DMA((len(arrays),))],
        compiler_params=pltpu.CompilerParams(vmem_limit_bytes=8 * 2**20),
    )(*arrays)


def per_device(
    time_count,
    group_count,
    cost,
    demand,
    conversion,
    upper,
    decay,
    energy_cap,
    annual_cap,
    line_ends,
    line_cap,
):
    f32, bf16 = jnp.float32, jnp.bfloat16
    hours, regions, width = cost.shape
    rows_bus = demand.shape[2]
    units = decay.shape[2]
    lines = line_ends.shape[0]
    rows = up_to(regions, 2 * SUBLANES)
    bus_width = up_to(regions * group_count, LANES)
    tiles = (rows // SUBLANES) * (width // LANES)
    share = -(-tiles // time_count) * SUBLANES
    vmem = pl.BlockSpec(memory_space=pltpu.VMEM)
    scratch = lambda *shape: pltpu.VMEM(shape, f32)
    half = lambda *shape: pltpu.VMEM(shape, bf16)
    flat = hours * regions
    by_region = lambda x: jnp.transpose(x, (1, 0, 2))
    operands = (
        by_region(cost),
        by_region(demand),
        conversion,
        upper,
        by_region(decay).reshape(flat, units),
        energy_cap,
        annual_cap,
        line_ends.T,
        line_cap.reshape(1, lines),
    )
    operands = tuple(pltpu.with_memory_space_constraint(x, pltpu.HBM) for x in operands)
    results = pl.pallas_call(
        functools.partial(kernel, time_count, group_count),
        out_shape=(
            jax.ShapeDtypeStruct((regions, hours, width), bf16),
            jax.ShapeDtypeStruct((hours, lines), f32),
            jax.ShapeDtypeStruct((regions, hours, rows_bus), f32),
            jax.ShapeDtypeStruct((flat, units), f32),
            jax.ShapeDtypeStruct((regions, width), f32),
        ),
        in_specs=[pl.BlockSpec(memory_space=pltpu.HBM)] * len(operands),
        out_specs=[vmem] * 5,
        scratch_shapes=[pltpu.VMEM(x.shape, x.dtype) for x in operands]
        + [
            half(width, rows_bus),
            half(width, rows_bus),
            half(flat, width),
            half(flat, width),
            half(flat, rows_bus),
            half(flat, rows_bus),
            scratch(flat, rows_bus),
            scratch(flat, rows_bus),
            scratch(flat, width),
            scratch(hours, regions, units),
            scratch(flat, units),
            scratch(hours, regions, units),
            scratch(hours, regions, units),
            scratch(flat, units),
            scratch(rows, width),
            scratch(rows, width),
            scratch(rows, width),
            scratch(time_count * group_count, 1, LANES),
            scratch(group_count, hours, bus_width),
            scratch(group_count, hours, bus_width),
            scratch(rows, units),
            scratch(time_count, rows, units),
            scratch(3, rows, units),
            scratch(3, time_count, rows, units),
            scratch(2, time_count, share, LANES),
            scratch(2, time_count, share, LANES),
            scratch(2, share, LANES),
            scratch(2, time_count, share, LANES),
            pltpu.SemaphoreType.DMA((8,)),
            pltpu.SemaphoreType.DMA((8,)),
            pltpu.SemaphoreType.DMA((3,)),
            pltpu.SemaphoreType.DMA((3,)),
            pltpu.SemaphoreType.DMA((9,)),
        ],
        compiler_params=pltpu.CompilerParams(
            collective_id=0, has_side_effects=True, vmem_limit_bytes=20 * 2**20
        ),
    )(*operands)
    primal, flows, prices, storage, year = delivered(results)
    return (
        by_region(primal),
        flows,
        by_region(prices),
        by_region(storage.reshape(regions, hours, units)),
        year,
    )


def solution(mesh):
    in_specs = (
        P("tm", "region", None),
        P("tm", "region", None),
        P(),
        P("region", None),
        P("tm", "region", None),
        P("region", None),
        P("region", None),
        P("region", None),
        P("region"),
    )
    out_specs = (
        P("tm", "region", None),
        P("tm", "region"),
        P("tm", "region", None),
        P("tm", "region", None),
        P("region", None),
    )
    return jax.shard_map(
        functools.partial(per_device, mesh.shape["tm"], mesh.shape["region"]),
        mesh=mesh,
        in_specs=in_specs,
        out_specs=out_specs,
        check_vma=False,
    )
```
